32 devices in a mesh: pipe: 2 (over y), tensor: 2 (over core), dp: 8 (over z, x).
Axes of the slice: x: 2, y: 2, z: 4, core: 2. Of those that a mesh axis runs over, the one named last changes fastest.
Arguments:
- images_in: bfloat16 [2, 8, 200, 768], P(None, 'dp', 'tensor'), may hold values from -6 to 6
- out_grad: bfloat16 [2, 8, 200, 768], P(None, 'dp', 'tensor'), may hold values from -6 to 6
- attn_gain: bfloat16 [2, 768], P('pipe', 'dp'), may hold values from 0.5 to 1.5
- attn_bias: bfloat16 [2, 768], P('pipe', 'dp'), may hold values from -3 to 3
- qkv_weight: bfloat16 [2, 3, 768, 768], P('pipe', None, 'dp', 'tensor'), may hold values from -0.3125 to 0.3125
- proj_weight: bfloat16 [2, 768, 768], P('pipe', 'tensor', 'dp'), may hold values from -0.3125 to 0.3125
- moe_gain: bfloat16 [2, 768], P('pipe', 'dp'), may hold values from 0.5 to 1.5
- moe_bias: bfloat16 [2, 768], P('pipe', 'dp'), may hold values from -3 to 3
- router_weight: bfloat16 [2, 768, 4], P('pipe', 'dp'), may hold values from -0.3125 to 0.3125
- inner_weight: bfloat16 [2, 4, 768, 3072], P('pipe', None, 'dp', 'tensor'), may hold values from -0.21875 to 0.21875
- outer_weight: bfloat16 [2, 4, 3072, 768], P('pipe', None, 'tensor', 'dp'), may hold values from -0.3125 to 0.3125
- expert_ids: int32 [2, 2, 8, 200, 2], P('pipe', None, 'dp'), may hold values from 0 to 3, as said below
- slot_ids: int32 [2, 2, 8, 200, 2], P('pipe', None, 'dp'), may hold values from 0 to 128, as said below
Outputs:
- activations: bfloat16 [2, 2, 8, 200, 768], P('pipe', None, 'dp', 'tensor')
- input_grads: float32 [2, 2, 8, 200, 768], P('pipe', None, 'dp', 'tensor')
- grad_attn_gain: float32 [2, 768], P('pipe', 'dp')
- grad_attn_bias: float32 [2, 768], P('pipe', 'dp')
- grad_qkv_weight: float32 [2, 3, 768, 768], P('pipe', None, 'dp', 'tensor')
- grad_proj_weight: float32 [2, 768, 768], P('pipe', 'tensor', 'dp')
- grad_moe_gain: float32 [2, 768], P('pipe', 'dp')
- grad_moe_bias: float32 [2, 768], P('pipe', 'dp')
- grad_router_weight: float32 [2, 768, 4], P('pipe', 'dp')
- grad_inner_weight: float32 [2, 4, 768, 3072], P('pipe', None, 'dp', 'tensor')
- grad_outer_weight: float32 [2, 4, 3072, 768], P('pipe', None, 'tensor', 'dp')
The draws below stay inside these ranges and needn't reach their ends.
Inputs may be any that keep to these rules, and one draw needn't show every extreme that they name: `expert_ids`: each token's two choices name different experts; in every image some expert is the first choice of 129 or more live tokens. `slot_ids`: A choice's slot is its rank among the image's choices of that expert by live tokens, all first choices in token order before all second choices; 128 marks a choice of rank 128 or more, or of a padding position. In every image some expert fills all 128 slots.
All inputs are finite; a program needn't handle non-finite values.
Results may differ from the reference program's by a relative error of at most 0.028.
Values may be sent and summed in bfloat16 or wider, within the bound.
A program may use at most 256 MiB of HBM per device.

```python
import jax
import jax.numpy as jnp
from jax import lax

D = 768
HEADS = 12
HEAD_DIM = 64
FF = 3072
LIVE = 197
SEQ = 200
EXPERTS = 4
CAP = 128
MB = 2
SECTIONS = 2
IMAGES = 8


def route_tables(key):
    base_key = jax.random.fold_in(key, 101)
    subkeys = jax.random.split(base_key, 4)
    lead_shape = (SECTIONS, MB, IMAGES)
    position = jnp.arange(SEQ, dtype=jnp.int32)
    live_mask = position < LIVE
    busy_expert = jax.random.randint(subkeys[0], lead_shape + (1,), 0, EXPERTS, dtype=jnp.int32)
    first_choice = jax.random.randint(subkeys[1], lead_shape + (SEQ,), 0, EXPERTS, dtype=jnp.int32)
    random_rank = jax.random.randint(subkeys[2], lead_shape + (SEQ,), 0, 4096, dtype=jnp.int32)
    order_key = jnp.where(live_mask, random_rank * SEQ + position, 4096 * SEQ + position)
    order_rank = jnp.argsort(jnp.argsort(order_key, axis=-1, stable=True), axis=-1, stable=True)
    first_choice = jnp.where(order_rank <= CAP, busy_expert, first_choice)
    offset = jax.random.randint(subkeys[3], lead_shape + (SEQ,), 1, EXPERTS, dtype=jnp.int32)
    second_choice = (first_choice + offset) % EXPERTS
    expert_cols = jnp.arange(EXPERTS, dtype=jnp.int32)
    ones_first = ((first_choice[..., None] == expert_cols) & live_mask[:, None]).astype(jnp.int32)
    ones_second = ((second_choice[..., None] == expert_cols) & live_mask[:, None]).astype(jnp.int32)
    before_first = jnp.cumsum(ones_first, axis=-2) - ones_first
    before_second = jnp.sum(ones_first, axis=-2, keepdims=True) + jnp.cumsum(ones_second, axis=-2) - ones_second
    rank_first = jnp.sum(before_first * ones_first, axis=-1)
    rank_second = jnp.sum(before_second * ones_second, axis=-1)
    slot_first = jnp.where(live_mask, jnp.minimum(rank_first, CAP), CAP)
    slot_second = jnp.where(live_mask, jnp.minimum(rank_second, CAP), CAP)
    return (jnp.stack([first_choice, second_choice], axis=-1), jnp.stack([slot_first, slot_second], axis=-1).astype(jnp.int32))


def draw_expert_ids(key, part):
    return route_tables(key)[0]


def draw_slot_ids(key, part):
    return route_tables(key)[1]


def spiked(values, own_key, source, target, parts, factor):
    def block_of(dim):
        return (jnp.arange(values.shape[dim]) // (values.shape[dim] // parts)).reshape((-1,) + (1,) * (values.ndim - 1 - dim))

    one_side = jax.random.permutation(own_key, parts)[block_of(target)]
    other_side = (block_of(target) + parts // 2) % parts
    return jnp.where((block_of(source) == one_side) | (block_of(source) == other_side), factor * values, values)


def level_of(rng, shape, shards, smallest, high):
    factor_of, own = 1.0, jax.random.fold_in(rng, 6)
    for axis_at, blocks in shards:
        heights = jnp.exp(jax.random.uniform(jax.random.fold_in(own, axis_at), (blocks,), jnp.float32, smallest / len(shards), high / len(shards)))
        factor_of = factor_of * jnp.repeat(heights, shape[axis_at] // blocks).reshape([-1 if axis == axis_at else 1 for axis in range(len(shape))])
    return factor_of


def normal_values(own_key, extent, width, limit, cuts=(), kind=jnp.bfloat16):
    array = jax.random.normal(own_key, extent, jnp.float32) * width
    if len(cuts) > 0:
        array = level_of(own_key, extent, cuts, -0.22, 0.18) * array
    return jnp.clip(array, min=-limit, max=limit).astype(kind)


def bell_draw_with(key, shape, width, limit, cuts, heavy, kind=jnp.bfloat16):
    array = width * jax.random.normal(key, shape, jnp.float32)
    if cuts:
        array = array * level_of(key, shape, cuts, -0.22, 0.18)
    return jnp.clip(spiked(array, jax.random.fold_in(key, 3), *heavy), -limit, limit).astype(kind)


def setup_inputs(seed: int = 0) -> dict:
    splits = jax.random.split(jax.random.key(seed), 14)
    images_in = normal_values(splits[0], (MB, IMAGES, SEQ, D), 1.0, 6.0, ((1, 8), (2, 2)))
    out_grad = bell_draw_with(splits[1], (MB, IMAGES, SEQ, D), 1.0, 6.0, ((1, 8), (2, 2)), (1, 3, 8, 2.0))
    attn_gain = jnp.clip(1.0 + 0.1 * jax.random.normal(splits[2], (SECTIONS, D), jnp.float32), 0.5, 1.5).astype(jnp.bfloat16)
    attn_bias = normal_values(splits[3], (SECTIONS, D), 0.5, 3.0, ((0, 2), (1, 8)))
    qkv_weight = normal_values(splits[4], (SECTIONS, 3, D, D), (D // 2) ** -0.5, 0.3125, ((0, 2), (2, 8), (3, 2)))
    proj_weight = normal_values(splits[5], (SECTIONS, D, D), (D // 2) ** -0.5, 0.3125, ((0, 2), (1, 2), (2, 8)))
    moe_gain = jnp.clip(1.0 + 0.1 * jax.random.normal(splits[6], (SECTIONS, D), jnp.float32), 0.5, 1.5).astype(jnp.bfloat16)
    moe_bias = normal_values(splits[7], (SECTIONS, D), 0.5, 3.0, ((0, 2), (1, 8)))
    router_weight = normal_values(splits[8], (SECTIONS, D, EXPERTS), (D // 2) ** -0.5, 0.3125, ((0, 2), (1, 8)))
    inner_weight = normal_values(splits[9], (SECTIONS, EXPERTS, D, FF), D ** -0.5, 0.21875, ((0, 2), (2, 8), (3, 2)))
    outer_weight = normal_values(splits[10], (SECTIONS, EXPERTS, FF, D), (FF // 8) ** -0.5, 0.3125, ((0, 2), (2, 2), (3, 8)))
    expert_ids = draw_expert_ids(jax.random.fold_in(splits[13], 71), 0)
    slot_ids = draw_slot_ids(jax.random.fold_in(splits[13], 71), 0)
    return dict(images_in=images_in, out_grad=out_grad, attn_gain=attn_gain, attn_bias=attn_bias, qkv_weight=qkv_weight, proj_weight=proj_weight, moe_gain=moe_gain, moe_bias=moe_bias, router_weight=router_weight, inner_weight=inner_weight, outer_weight=outer_weight, expert_ids=expert_ids, slot_ids=slot_ids)


@jax.custom_vjp
def low(v):
    return lax.optimization_barrier(v.astype(jnp.bfloat16)).astype(jnp.float32)

@jax.custom_vjp
def low_back(v):
    return v

def low_keep(v):
    return (low(v), None)

def low_pass(kept, grad):
    return (grad,)

def back_keep(v):
    return (v, None)

def back_low(kept, grad):
    return (low(grad),)
low.defvjp(low_keep, low_pass)
low_back.defvjp(back_keep, back_low)
highest = lax.Precision.HIGHEST
epsilon = 1e-06

def layer_norm(values, norm_gain, norm_bias):
    centre = values - lax.optimization_barrier(jnp.mean(values, axis=-1, keepdims=True))
    spread = lax.optimization_barrier(jnp.mean(centre * centre, axis=-1, keepdims=True))
    return centre * lax.rsqrt(spread + epsilon) * norm_gain + norm_bias

def image_layer(params, pieces):
    attn_gain, attn_bias, qkv_weight, proj_weight, moe_gain, moe_bias, router_weight, inner_weight, outer_weight = params
    tokens, route_ids, slot_ids = pieces
    length = tokens.shape[0]
    normed = low(layer_norm(tokens, attn_gain, attn_bias))
    projected = jnp.einsum('sd,jde->jse', normed, qkv_weight, precision=highest)
    query_rows = low_back(low(projected[0])).reshape(length, HEADS, HEAD_DIM)
    key_rows = low_back(low(projected[1])).reshape(length, HEADS, HEAD_DIM)
    value_rows = low_back(low(projected[2])).reshape(length, HEADS, HEAD_DIM)
    scores = low_back(jnp.einsum('qhd,khd->hqk', query_rows, key_rows, precision=highest) * HEAD_DIM ** (-0.5))
    live_keys = jnp.arange(length) < LIVE
    scores = jnp.where(live_keys, scores, -1e+30)
    attention = jax.nn.softmax(scores, axis=-1)
    attended = jnp.einsum('hqk,khd->qhd', low(attention), value_rows, precision=highest).reshape(length, HEADS * HEAD_DIM)
    attended = low_back(low(attended))
    branch = low_back(jnp.dot(attended, proj_weight, precision=highest))
    hidden = tokens + branch
    normed_two = low(layer_norm(hidden, moe_gain, moe_bias))
    router_probs = jax.nn.softmax(jnp.dot(normed_two, router_weight, precision=highest), axis=-1)
    columns = jnp.arange(EXPERTS * CAP, dtype=jnp.int32)
    slot_codes = jnp.where(slot_ids < CAP, route_ids * CAP + slot_ids, -1)
    picked = (slot_codes[:, :, None] == columns).astype(jnp.float32)
    expert_hot = (route_ids[:, :, None] == jnp.arange(EXPERTS, dtype=jnp.int32)).astype(jnp.float32)
    gate_values = lax.optimization_barrier(jnp.sum(router_probs[:, None, :] * expert_hot, axis=-1))
    dispatch = lax.optimization_barrier(jnp.sum(picked, axis=1))
    combine = lax.optimization_barrier(jnp.sum(picked * gate_values[:, :, None], axis=1))
    expert_rows = jnp.dot(dispatch.T, normed_two, precision=highest).reshape(EXPERTS, CAP, D)
    pre_act = low_back(jnp.einsum('ecd,edf->ecf', expert_rows, inner_weight, precision=highest))
    activated = low(jax.nn.gelu(pre_act, approximate=True))
    expert_out = low_back(jnp.einsum('ecf,efd->ecd', activated, outer_weight, precision=highest))
    moe_out = jnp.dot(combine, expert_out.reshape(EXPERTS * CAP, D), precision=highest)
    return hidden + moe_out

def run_section(params, section_in, route_ids, slot_ids):
    checked = jax.checkpoint(image_layer)

    def scan_step(carry_in, pieces):
        return (carry_in, checked(params, pieces))
    carry_out, results = lax.scan(scan_step, jnp.zeros((), jnp.float32), (section_in, route_ids, slot_ids))
    return results

def forward(shift_all, params_all, images, route_all, slot_all):
    section_outputs = [[] for section_index in range(SECTIONS)]
    for mb_index in range(MB):
        section_in = images[mb_index]
        for section_index in range(SECTIONS):
            params = tuple((member[section_index] for member in params_all))
            result = run_section(params, section_in + shift_all[section_index, mb_index], route_all[section_index, mb_index], slot_all[section_index, mb_index])
            section_outputs[section_index].append(low(result))
            section_in = low_back(low(result))
    return jnp.stack([jnp.stack(per_section) for per_section in section_outputs])

def reference(images_in, out_grad, attn_gain, attn_bias, qkv_weight, proj_weight, moe_gain, moe_bias, router_weight, inner_weight, outer_weight, expert_ids, slot_ids):
    params_all = tuple((weight_array.astype(jnp.float32) for weight_array in (attn_gain, attn_bias, qkv_weight, proj_weight, moe_gain, moe_bias, router_weight, inner_weight, outer_weight)))
    images = images_in.astype(jnp.float32)
    shift_zero = jnp.zeros((SECTIONS,) + images.shape, jnp.float32)

    def whole_pass(shift_all, params_given):
        return forward(shift_all, params_given, images, expert_ids, slot_ids)
    activations, pull_back = jax.vjp(whole_pass, shift_zero, params_all)
    cotangent = jnp.zeros_like(activations).at[SECTIONS - 1].set(out_grad.astype(jnp.float32))
    grad_shift, grad_params = pull_back(cotangent)
    return (activations.astype(jnp.bfloat16), grad_shift, grad_params[0], grad_params[1], grad_params[2], grad_params[3], grad_params[4], grad_params[5], grad_params[6], grad_params[7], grad_params[8])
```

```python
import jax
import jax.numpy as jnp
from jax import lax
from jax.sharding import PartitionSpec as P

HEAD_DIM = 64
LIVE = 197
CAP = 128
ROWS = 128
EPS = 1e-06
BF = jnp.bfloat16
F32 = jnp.float32


def dot(spec, left, right):
    return jnp.einsum(spec, left, right, preferred_element_type=F32)


def swap(values):
    return lax.ppermute(values, "tensor", [(0, 1), (1, 0)])


def join_halves(own):
    return jnp.concatenate([own, swap(own)], axis=1)


def sum_halves(full, wire):
    rows = full.shape[1] // 2
    return full[:, :rows].astype(F32) + swap(full[:, rows:].astype(wire)).astype(F32)


def norm_stats(values):
    centre = values - jnp.mean(values, axis=-1, keepdims=True)
    inv = lax.rsqrt(jnp.mean(centre * centre, axis=-1, keepdims=True) + EPS)
    return centre * inv, inv


def norm_back(grad, unit, inv, gain):
    scaled = grad * gain
    return (
        scaled
        - jnp.mean(scaled, axis=-1, keepdims=True)
        - unit * jnp.mean(scaled * unit, axis=-1, keepdims=True)
    ) * inv


def gelu_parts(pre):
    inner = 0.7978845608028654 * (pre + 0.044715 * pre * pre * pre)
    return jnp.tanh(inner)


def forward(section_input, weights, tables):
    gain1, bias1, gain2, bias2, qkv, projt, router, inner, outert = weights
    onehot, kept, hot, key_live, = tables
    images, rows, features = section_input.shape
    length = 2 * rows
    experts = router.shape[1]
    heads = qkv.shape[2] // HEAD_DIM
    z = section_input.astype(F32)
    unit1, inv1 = norm_stats(z)
    a1 = join_halves((unit1 * gain1 + bias1).astype(BF))
    qkv_rows = dot("isd,jde->jise", a1, qkv).astype(BF)
    q, k, v = (qkv_rows[j].reshape(images, length, heads, HEAD_DIM) for j in range(3))
    scores = dot("iqhd,ikhd->ihqk", q, k) * HEAD_DIM**-0.5
    scores = jnp.where(key_live, scores, -1e30)
    top = jnp.max(scores, axis=-1, keepdims=True)
    weights_exp = jnp.exp(scores - top)
    probs = weights_exp / jnp.sum(weights_exp, axis=-1, keepdims=True)
    attended = dot("ihqk,ikhd->iqhd", probs.astype(BF), v).astype(BF)
    attended = attended.reshape(images, length, heads * HEAD_DIM)
    h1 = z + sum_halves(dot("ise,de->isd", attended, projt), F32)
    unit2, inv2 = norm_stats(h1)
    a2 = join_halves((unit2 * gain2 + bias2).astype(BF))
    router_probs = jax.nn.softmax(dot("isd,de->ise", a2, router), axis=-1)
    gate = jnp.sum(jnp.where(hot, router_probs[:, None], 0.0), axis=-1)
    dispatch = onehot[:, 0] + onehot[:, 1]
    rows_e = dot("isc,isd->icd", dispatch, a2).astype(BF)
    rows_e = rows_e.reshape(images, experts, CAP, features).transpose(1, 0, 2, 3)
    rows_e = rows_e.reshape(experts, images * CAP, features)
    pre = dot("ecd,edf->ecf", rows_e, inner)
    act = (0.5 * pre * (1.0 + gelu_parts(pre))).astype(BF)
    out = dot("ecf,edf->ecd", act, outert).astype(BF)
    out = out.reshape(experts, images, CAP, features).transpose(1, 0, 2, 3)
    out = out.reshape(images, experts * CAP, features)
    chosen = dot("iksc,icd->iksd", onehot, out)
    moe = jnp.sum(chosen * gate[..., None], axis=1)
    y = h1 + sum_halves(moe, F32)
    saved = (unit1, inv1, a1, q, k, v, probs, attended, unit2, inv2, a2, router_probs, gate,
             rows_e, pre, act, chosen.astype(BF))
    return y.astype(BF), saved


def backward(dy, saved, weights, tables):
    gain1, bias1, gain2, bias2, qkv, projt, router, inner, outert = weights
    onehot, kept, hot, key_live, = tables
    (unit1, inv1, a1, q, k, v, probs, attended, unit2, inv2, a2, router_probs, gate,
     rows_e, pre, act, chosen) = saved
    images, rows, features = dy.shape
    length = 2 * rows
    experts = router.shape[1]
    heads = qkv.shape[2] // HEAD_DIM
    scale = HEAD_DIM**-0.5
    grad_full = join_halves(dy).astype(F32)
    weighted = (gate[..., None] * grad_full[:, None]).astype(BF)
    dexp = dot("iksc,iksd->icd", onehot, weighted).astype(BF)
    dexp = dexp.reshape(images, experts, CAP, features).transpose(1, 0, 2, 3)
    dexp = dexp.reshape(experts, images * CAP, features)
    grad_outert = dot("ecd,ecf->edf", dexp, act).astype(BF)
    grad_act = dot("ecd,edf->ecf", dexp, outert)
    tanh = gelu_parts(pre)
    slope = 0.5 * (1.0 + tanh) + 0.5 * pre * (1.0 - tanh * tanh) * (
        0.7978845608028654 * (1.0 + 3 * 0.044715 * pre * pre)
    )
    dpre = (grad_act * slope).astype(BF)
    grad_inner = dot("ecd,ecf->edf", rows_e, dpre).astype(BF)
    drows = dot("ecf,edf->ecd", dpre, inner).astype(BF)
    drows = drows.reshape(experts, images, CAP, features).transpose(1, 0, 2, 3)
    drows = drows.reshape(images, experts * CAP, features)
    dgate = jnp.where(kept, jnp.sum(grad_full[:, None] * chosen.astype(F32), axis=-1), 0.0)
    drouter = jnp.sum(jnp.where(hot, dgate[..., None], 0.0), axis=1)
    dlogit = router_probs * (drouter - jnp.sum(router_probs * drouter, axis=-1, keepdims=True))
    grad_router = jnp.einsum(
        "isd,ise->de", a2.astype(F32), dlogit, precision=lax.Precision.HIGHEST
    )
    da2 = jnp.einsum("ise,de->isd", dlogit, router.astype(F32), precision=lax.Precision.HIGHEST)
    da2 = da2 + dot("isc,icd->isd", onehot[:, 0] + onehot[:, 1], drows)
    da2 = sum_halves(da2, BF)
    grad_gain2 = jnp.sum(da2 * unit2, axis=(0, 1))
    grad_bias2 = jnp.sum(da2, axis=(0, 1))
    dh1 = dy.astype(F32) + norm_back(da2, unit2, inv2, gain2)
    dbranch = join_halves(dh1.astype(BF))
    grad_projt = dot("isd,ise->de", dbranch, attended).astype(BF)
    datt = dot("isd,de->ise", dbranch, projt).astype(BF)
    datt = datt.reshape(images, length, heads, HEAD_DIM)
    dv = dot("ihqk,iqhd->ikhd", probs.astype(BF), datt).astype(BF)
    dprobs = dot("iqhd,ikhd->ihqk", datt, v)
    dscores = probs * (dprobs - jnp.sum(probs * dprobs, axis=-1, keepdims=True))
    dscores = dscores.astype(BF)
    dq = (dot("ihqk,ikhd->iqhd", dscores, k) * scale).astype(BF)
    dk = (dot("ihqk,iqhd->ikhd", dscores, q) * scale).astype(BF)
    flat = tuple(part.reshape(images, length, heads * HEAD_DIM) for part in (dq, dk, dv))
    grad_qkv = tuple(dot("isd,ise->de", a1, part).astype(BF) for part in flat)
    da1 = sum(dot("ise,de->isd", part, qkv[j]) for j, part in enumerate(flat))
    da1 = sum_halves(da1, BF)
    grad_gain1 = jnp.sum(da1 * unit1, axis=(0, 1))
    grad_bias1 = jnp.sum(da1, axis=(0, 1))
    dz = dh1 + norm_back(da1, unit1, inv1, gain1)
    small = jnp.concatenate(
        [jnp.stack([grad_gain1, grad_bias1, grad_gain2, grad_bias2], axis=1), grad_router], axis=1
    )
    return dz, grad_qkv, grad_projt, small, grad_inner, grad_outert


def gather_dp(shard):
    return lax.all_gather(shard, "dp", axis=shard.ndim - 2, tiled=True)


def scatter_dp(full):
    return lax.psum_scatter(full, "dp", scatter_dimension=full.ndim - 2, tiled=True)


def body(
    images_in,
    out_grad,
    attn_gain,
    attn_bias,
    qkv_weight,
    proj_weight,
    moe_gain,
    moe_bias,
    router_weight,
    inner_weight,
    outer_weight,
    expert_ids,
    slot_ids,
):
    is_first = lax.axis_index("pipe") == 0
    side = lax.axis_index("tensor")
    micro, local, piece, features = images_in.shape
    images = micro * local
    shard, wide = qkv_weight.shape[2], qkv_weight.shape[3]
    experts = router_weight.shape[2]
    packed = jnp.concatenate(
        [qkv_weight[0, 0], qkv_weight[0, 1], qkv_weight[0, 2], proj_weight[0].T,
         jnp.stack([attn_gain[0], attn_bias[0], moe_gain[0], moe_bias[0]], axis=1),
         router_weight[0], jnp.zeros((shard, 128 - 4 - experts), BF)],
        axis=1,
    )
    packed = gather_dp(packed)
    inner = gather_dp(inner_weight)[0]
    outert = gather_dp(outer_weight.transpose(0, 1, 3, 2))[0]
    qkv = jnp.stack([packed[:, j * wide:(j + 1) * wide] for j in range(3)])
    projt = packed[:, 3 * wide:4 * wide]
    smalls = packed[:, 4 * wide:]
    gain1, bias1, gain2, bias2 = (smalls[:, j].astype(F32) for j in range(4))
    router = smalls[:, 4:4 + experts]
    weights = (gain1, bias1, gain2, bias2, qkv, projt, router, inner, outert)

    def pad_rows(values, fill=0):
        return jnp.pad(
            values, ((0, 0), (0, ROWS - piece), (0, 0)), constant_values=fill
        )

    def local_order(table, fill):
        halves = table[0].reshape(images, 2, piece, 2)
        halves = jnp.where(side == 0, halves, halves[:, ::-1])
        halves = jnp.pad(
            halves, ((0, 0), (0, 0), (0, ROWS - piece), (0, 0)), constant_values=fill
        )
        return halves.reshape(images, 2 * ROWS, 2).transpose(0, 2, 1)

    routes = local_order(expert_ids, 0)
    slots = local_order(slot_ids, CAP)
    kept = slots < CAP
    codes = jnp.where(kept, routes * CAP + slots, -1)
    onehot = (codes[..., None] == jnp.arange(experts * CAP, dtype=jnp.int32)).astype(BF)
    hot = routes[..., None] == jnp.arange(experts, dtype=jnp.int32)
    index = jnp.arange(2 * ROWS, dtype=jnp.int32)
    half = jnp.where(side == 0, index // ROWS, 1 - index // ROWS)
    row = index % ROWS
    key_live = (row < piece) & (half * piece + row < LIVE)
    tables = (onehot, kept, hot, key_live)

    start = pad_rows(images_in.reshape(images, piece, features))
    last = pad_rows(out_grad.reshape(images, piece, features))
    early, _ = forward(start, weights, tables)
    received = lax.ppermute(early, "pipe", [(0, 1)])
    y, saved = forward(jnp.where(is_first, start, received), weights, tables)
    late = backward(last, saved, weights, tables)[0]
    received = lax.ppermute(late.astype(BF), "pipe", [(1, 0)])
    dz, grad_qkv, grad_projt, small, grad_inner, grad_outert = backward(
        jnp.where(is_first, received, last), saved, weights, tables
    )
    outer_out = scatter_dp(grad_outert[None])
    inner_out = scatter_dp(grad_inner[None])
    packed_grads = jnp.concatenate(
        [*grad_qkv, grad_projt, small.astype(BF),
         jnp.zeros((features, 128 - small.shape[1]), BF)],
        axis=1,
    )
    packed_out = scatter_dp(packed_grads).astype(F32)
    own_small = packed_out[:, 4 * wide:4 * wide + small.shape[1]]
    own_small = own_small + swap(own_small)

    def shape_out(values):
        return values[:, :piece].reshape(1, micro, local, piece, features)

    return (
        shape_out(y),
        shape_out(dz),
        own_small[:, 0][None],
        own_small[:, 1][None],
        jnp.stack([packed_out[:, j * wide:(j + 1) * wide] for j in range(3)])[None],
        packed_out[:, 3 * wide:4 * wide].T[None],
        own_small[:, 2][None],
        own_small[:, 3][None],
        own_small[:, 4:][None],
        inner_out.astype(F32),
        outer_out.astype(F32).transpose(0, 1, 3, 2),
    )


def solution(mesh):
    in_specs = (
        P(None, "dp", "tensor", None),
        P(None, "dp", "tensor", None),
        P("pipe", "dp"),
        P("pipe", "dp"),
        P("pipe", None, "dp", "tensor"),
        P("pipe", "tensor", "dp"),
        P("pipe", "dp"),
        P("pipe", "dp"),
        P("pipe", "dp", None),
        P("pipe", None, "dp", "tensor"),
        P("pipe", None, "tensor", "dp"),
        P("pipe", None, "dp", None, None),
        P("pipe", None, "dp", None, None),
    )
    out_specs = (
        P("pipe", None, "dp", "tensor", None),
        P("pipe", None, "dp", "tensor", None),
        P("pipe", "dp"),
        P("pipe", "dp"),
        P("pipe", None, "dp", "tensor"),
        P("pipe", "tensor", "dp"),
        P("pipe", "dp"),
        P("pipe", "dp"),
        P("pipe", "dp", None),
        P("pipe", None, "dp", "tensor"),
        P("pipe", None, "tensor", "dp"),
    )
    return jax.shard_map(body, mesh=mesh, in_specs=in_specs, out_specs=out_specs, check_vma=False)
```

```python
import jax
import jax.numpy as jnp
import numpy as np
from jax import lax
from jax.sharding import PartitionSpec as P

HEAD_DIM = 64
LIVE = 197
CAP = 128
ROWS = 128
STREAMS = 2
EPS = 1e-06
BF = jnp.bfloat16
F32 = jnp.float32


def dot(spec, left, right):
    return jnp.einsum(spec, left, right, preferred_element_type=F32)


def swap(values):
    return lax.ppermute(values, "tensor", [(0, 1), (1, 0)])


def join_halves(own):
    return jnp.concatenate([own, swap(own)], axis=1)


def sum_halves(full, wire):
    rows = full.shape[1] // 2
    return full[:, :rows].astype(F32) + swap(full[:, rows:].astype(wire)).astype(F32)


def norm_stats(values):
    centre = values - jnp.mean(values, axis=-1, keepdims=True)
    inv = lax.rsqrt(jnp.mean(centre * centre, axis=-1, keepdims=True) + EPS)
    return centre * inv, inv


def norm_back(grad, unit, inv, gain):
    scaled = grad * gain
    return (
        scaled
        - jnp.mean(scaled, axis=-1, keepdims=True)
        - unit * jnp.mean(scaled * unit, axis=-1, keepdims=True)
    ) * inv


def gelu_parts(pre):
    inner = 0.7978845608028654 * (pre + 0.044715 * pre * pre * pre)
    return jnp.tanh(inner)


def forward(section_input, weights, tables):
    gain1, bias1, gain2, bias2, qkv, projt, router, inner, outert = weights
    onehot, kept, hot, key_live, = tables
    images, rows, features = section_input.shape
    length = 2 * rows
    experts = router.shape[1]
    heads = qkv.shape[2] // HEAD_DIM
    z = section_input.astype(F32)
    unit1, inv1 = norm_stats(z)
    a1 = join_halves((unit1 * gain1 + bias1).astype(BF))
    qkv_rows = dot("isd,jde->jise", a1, qkv).astype(BF)
    q, k, v = (qkv_rows[j].reshape(images, length, heads, HEAD_DIM) for j in range(3))
    scores = dot("iqhd,ikhd->ihqk", q, k) * HEAD_DIM**-0.5
    scores = jnp.where(key_live, scores, -1e30)
    top = jnp.max(scores, axis=-1, keepdims=True)
    weights_exp = jnp.exp(scores - top)
    probs = weights_exp / jnp.sum(weights_exp, axis=-1, keepdims=True)
    attended = dot("ihqk,ikhd->iqhd", probs.astype(BF), v).astype(BF)
    attended = attended.reshape(images, length, heads * HEAD_DIM)
    h1 = z + sum_halves(dot("ise,de->isd", attended, projt), F32)
    unit2, inv2 = norm_stats(h1)
    a2 = join_halves((unit2 * gain2 + bias2).astype(BF))
    router_probs = jax.nn.softmax(dot("isd,de->ise", a2, router), axis=-1)
    gate = jnp.sum(jnp.where(hot, router_probs[:, None], 0.0), axis=-1)
    dispatch = onehot[:, 0] + onehot[:, 1]
    rows_e = dot("isc,isd->icd", dispatch, a2).astype(BF)
    rows_e = rows_e.reshape(images, experts, CAP, features).transpose(1, 0, 2, 3)
    rows_e = rows_e.reshape(experts, images * CAP, features)
    pre = dot("ecd,edf->ecf", rows_e, inner)
    act = (0.5 * pre * (1.0 + gelu_parts(pre))).astype(BF)
    out = dot("ecf,edf->ecd", act, outert).astype(BF)
    out = out.reshape(experts, images, CAP, features).transpose(1, 0, 2, 3)
    out = out.reshape(images, experts * CAP, features)
    chosen = dot("iksc,icd->iksd", onehot, out)
    moe = jnp.sum(chosen * gate[..., None], axis=1)
    y = h1 + sum_halves(moe, F32)
    saved = (unit1, inv1, a1, q, k, v, probs, attended, unit2, inv2, a2, router_probs, gate,
             rows_e, pre, act, chosen.astype(BF))
    return y.astype(BF), saved


def backward(dy, saved, weights, tables, weight_grads):
    gain1, bias1, gain2, bias2, qkv, projt, router, inner, outert = weights
    onehot, kept, hot, key_live, = tables
    (unit1, inv1, a1, q, k, v, probs, attended, unit2, inv2, a2, router_probs, gate,
     rows_e, pre, act, chosen) = saved
    images, rows, features = dy.shape
    length = 2 * rows
    experts = router.shape[1]
    heads = qkv.shape[2] // HEAD_DIM
    scale = HEAD_DIM**-0.5
    grad_full = join_halves(dy).astype(F32)
    weighted = (gate[..., None] * grad_full[:, None]).astype(BF)
    dexp = dot("iksc,iksd->icd", onehot, weighted).astype(BF)
    dexp = dexp.reshape(images, experts, CAP, features).transpose(1, 0, 2, 3)
    dexp = dexp.reshape(experts, images * CAP, features)
    grad_outert = dot("ecd,ecf->edf", dexp, act).astype(BF)
    if weight_grads:
        grad_outert, dexp = lax.optimization_barrier((grad_outert, dexp))
    grad_act = dot("ecd,edf->ecf", dexp, outert)
    tanh = gelu_parts(pre)
    slope = 0.5 * (1.0 + tanh) + 0.5 * pre * (1.0 - tanh * tanh) * (
        0.7978845608028654 * (1.0 + 3 * 0.044715 * pre * pre)
    )
    dpre = (grad_act * slope).astype(BF)
    grad_inner = dot("ecd,ecf->edf", rows_e, dpre).astype(BF)
    if weight_grads:
        grad_inner, dpre = lax.optimization_barrier((grad_inner, dpre))
    drows = dot("ecf,edf->ecd", dpre, inner).astype(BF)
    drows = drows.reshape(experts, images, CAP, features).transpose(1, 0, 2, 3)
    drows = drows.reshape(images, experts * CAP, features)
    dgate = jnp.where(kept, jnp.sum(grad_full[:, None] * chosen.astype(F32), axis=-1), 0.0)
    drouter = jnp.sum(jnp.where(hot, dgate[..., None], 0.0), axis=1)
    dlogit = router_probs * (drouter - jnp.sum(router_probs * drouter, axis=-1, keepdims=True))
    grad_router = jnp.einsum(
        "isd,ise->de", a2.astype(F32), dlogit, precision=lax.Precision.HIGHEST
    )
    da2 = jnp.einsum("ise,de->isd", dlogit, router.astype(F32), precision=lax.Precision.HIGHEST)
    da2 = da2 + dot("isc,icd->isd", onehot[:, 0] + onehot[:, 1], drows)
    da2 = sum_halves(da2, BF)
    grad_gain2 = jnp.sum(da2 * unit2, axis=(0, 1))
    grad_bias2 = jnp.sum(da2, axis=(0, 1))
    dh1 = dy.astype(F32) + norm_back(da2, unit2, inv2, gain2)
    dbranch = join_halves(dh1.astype(BF))
    grad_projt = dot("isd,ise->de", dbranch, attended).astype(BF)
    datt = dot("isd,de->ise", dbranch, projt).astype(BF)
    datt = datt.reshape(images, length, heads, HEAD_DIM)
    dv = dot("ihqk,iqhd->ikhd", probs.astype(BF), datt).astype(BF)
    dprobs = dot("iqhd,ikhd->ihqk", datt, v)
    dscores = probs * (dprobs - jnp.sum(probs * dprobs, axis=-1, keepdims=True))
    dscores = dscores.astype(BF)
    dq = (dot("ihqk,ikhd->iqhd", dscores, k) * scale).astype(BF)
    dk = (dot("ihqk,iqhd->ikhd", dscores, q) * scale).astype(BF)
    flat = tuple(part.reshape(images, length, heads * HEAD_DIM) for part in (dq, dk, dv))
    grad_qkv = tuple(dot("isd,ise->de", a1, part).astype(BF) for part in flat)
    da1 = sum(dot("ise,de->isd", part, qkv[j]) for j, part in enumerate(flat))
    da1 = sum_halves(da1, BF)
    grad_gain1 = jnp.sum(da1 * unit1, axis=(0, 1))
    grad_bias1 = jnp.sum(da1, axis=(0, 1))
    dz = dh1 + norm_back(da1, unit1, inv1, gain1)
    small = jnp.concatenate(
        [jnp.stack([grad_gain1, grad_bias1, grad_gain2, grad_bias2], axis=1), grad_router], axis=1
    )
    return dz, grad_qkv, grad_projt, small, grad_inner, grad_outert


def gather_dp(shard):
    return lax.all_gather(shard, "dp", axis=shard.ndim - 2, tiled=True)


def scatter_dp(full):
    return lax.psum_scatter(full, "dp", scatter_dimension=full.ndim - 2, tiled=True)


def ring_plan(count, forward_way):
    order = list(range(0, count, 2)) + list(range(count - 1 - count % 2, 0, -2))
    if not forward_way:
        order = order[::-1]
    links = [(order[i], order[(i + 1) % count]) for i in range(count)]
    behind = np.zeros((count, count), np.int32)
    for place, device in enumerate(order):
        for steps in range(count):
            behind[device, steps] = order[(place - steps) % count]
    row = jnp.asarray(behind)[lax.axis_index("dp")]
    return links, [row[steps] for steps in range(count)]


def ring_gather(shard, forward_way):
    count = lax.axis_size("dp")
    links, behind = ring_plan(count, forward_way)
    experts, depth, wide = shard.shape
    moving = shard[:, None]
    whole = jnp.zeros((experts, count, depth, wide), shard.dtype)
    whole = lax.dynamic_update_slice_in_dim(whole, moving, behind[0], 1)
    for step in range(1, count):
        moving = lax.ppermute(moving, "dp", links)
        whole = lax.dynamic_update_slice_in_dim(whole, moving, behind[step], 1)
    return whole.reshape(experts, count * depth, wide)


def ring_scatter(full, forward_way, streams):
    count = lax.axis_size("dp")
    links, behind = ring_plan(count, forward_way)
    experts, depth, wide = full.shape
    blocks = full.reshape(experts, count, depth // count, wide)
    part = experts // streams
    done = []
    for stream in range(streams):
        mine = blocks[stream * part:(stream + 1) * part]
        moving = lax.dynamic_index_in_dim(mine, behind[1 % count], 1, keepdims=False)
        for step in range(2, count + 1):
            came = lax.ppermute(moving, "dp", links).astype(F32)
            own = lax.dynamic_index_in_dim(mine, behind[step % count], 1, keepdims=False)
            moving = came + own.astype(F32)
            if step < count:
                moving = moving.astype(BF)
        done.append(moving.astype(F32))
    return jnp.concatenate(done, axis=0)


def body(
    images_in,
    out_grad,
    attn_gain,
    attn_bias,
    qkv_weight,
    proj_weight,
    moe_gain,
    moe_bias,
    router_weight,
    inner_weight,
    outer_weight,
    expert_ids,
    slot_ids,
):
    is_first = lax.axis_index("pipe") == 0
    side = lax.axis_index("tensor")
    micro, local, piece, features = images_in.shape
    images = micro * local
    shard, wide = qkv_weight.shape[2], qkv_weight.shape[3]
    experts = router_weight.shape[2]
    packed = jnp.concatenate(
        [qkv_weight[0, 0], qkv_weight[0, 1], qkv_weight[0, 2], proj_weight[0].T,
         jnp.stack([attn_gain[0], attn_bias[0], moe_gain[0], moe_bias[0]], axis=1),
         router_weight[0], jnp.zeros((shard, 128 - 4 - experts), BF)],
        axis=1,
    )
    packed = gather_dp(packed)
    inner = ring_gather(inner_weight[0], True)
    outert = ring_gather(outer_weight[0].transpose(0, 2, 1), False)
    qkv = jnp.stack([packed[:, j * wide:(j + 1) * wide] for j in range(3)])
    projt = packed[:, 3 * wide:4 * wide]
    smalls = packed[:, 4 * wide:]
    gain1, bias1, gain2, bias2 = (smalls[:, j].astype(F32) for j in range(4))
    router = smalls[:, 4:4 + experts]
    weights = (gain1, bias1, gain2, bias2, qkv, projt, router, inner, outert)

    def pad_rows(values, fill=0):
        return jnp.pad(
            values, ((0, 0), (0, ROWS - piece), (0, 0)), constant_values=fill
        )

    def local_order(table, fill):
        halves = table[0].reshape(images, 2, piece, 2)
        halves = jnp.where(side == 0, halves, halves[:, ::-1])
        halves = jnp.pad(
            halves, ((0, 0), (0, 0), (0, ROWS - piece), (0, 0)), constant_values=fill
        )
        return halves.reshape(images, 2 * ROWS, 2).transpose(0, 2, 1)

    routes = local_order(expert_ids, 0)
    slots = local_order(slot_ids, CAP)
    kept = slots < CAP
    codes = jnp.where(kept, routes * CAP + slots, -1)
    onehot = (codes[..., None] == jnp.arange(experts * CAP, dtype=jnp.int32)).astype(BF)
    hot = routes[..., None] == jnp.arange(experts, dtype=jnp.int32)
    index = jnp.arange(2 * ROWS, dtype=jnp.int32)
    half = jnp.where(side == 0, index // ROWS, 1 - index // ROWS)
    row = index % ROWS
    key_live = (row < piece) & (half * piece + row < LIVE)
    tables = (onehot, kept, hot, key_live)

    start = pad_rows(images_in.reshape(images, piece, features))
    last = pad_rows(out_grad.reshape(images, piece, features))
    early, _ = forward(start, weights, tables)
    received = lax.ppermute(early, "pipe", [(0, 1)])
    y, saved = forward(jnp.where(is_first, start, received), weights, tables)
    late = backward(last, saved, weights, tables, False)[0]
    received = lax.ppermute(late.astype(BF), "pipe", [(1, 0)])
    dz, grad_qkv, grad_projt, small, grad_inner, grad_outert = backward(
        jnp.where(is_first, received, last), saved, weights, tables, True
    )
    outer_out = ring_scatter(grad_outert, False, STREAMS)
    inner_out = ring_scatter(grad_inner, True, STREAMS)
    packed_grads = jnp.concatenate(
        [*grad_qkv, grad_projt, small.astype(BF),
         jnp.zeros((features, 128 - small.shape[1]), BF)],
        axis=1,
    )
    packed_out = scatter_dp(packed_grads).astype(F32)
    own_small = packed_out[:, 4 * wide:4 * wide + small.shape[1]]
    own_small = own_small + swap(own_small)

    def shape_out(values):
        return values[:, :piece].reshape(1, micro, local, piece, features)

    return (
        shape_out(y),
        shape_out(dz),
        own_small[:, 0][None],
        own_small[:, 1][None],
        jnp.stack([packed_out[:, j * wide:(j + 1) * wide] for j in range(3)])[None],
        packed_out[:, 3 * wide:4 * wide].T[None],
        own_small[:, 2][None],
        own_small[:, 3][None],
        own_small[:, 4:][None],
        inner_out[None],
        outer_out.transpose(0, 2, 1)[None],
    )


def solution(mesh):
    in_specs = (
        P(None, "dp", "tensor", None),
        P(None, "dp", "tensor", None),
        P("pipe", "dp"),
        P("pipe", "dp"),
        P("pipe", None, "dp", "tensor"),
        P("pipe", "tensor", "dp"),
        P("pipe", "dp"),
        P("pipe", "dp"),
        P("pipe", "dp", None),
        P("pipe", None, "dp", "tensor"),
        P("pipe", None, "tensor", "dp"),
        P("pipe", None, "dp", None, None),
        P("pipe", None, "dp", None, None),
    )
    out_specs = (
        P("pipe", None, "dp", "tensor", None),
        P("pipe", None, "dp", "tensor", None),
        P("pipe", "dp"),
        P("pipe", "dp"),
        P("pipe", None, "dp", "tensor"),
        P("pipe", "tensor", "dp"),
        P("pipe", "dp"),
        P("pipe", "dp"),
        P("pipe", "dp", None),
        P("pipe", None, "dp", "tensor"),
        P("pipe", None, "tensor", "dp"),
    )
    return jax.shard_map(body, mesh=mesh, in_specs=in_specs, out_specs=out_specs, check_vma=False)
```

```python
import jax
import jax.numpy as jnp
import numpy as np
from jax import lax
from jax.sharding import PartitionSpec as P

HEAD_DIM = 64
LIVE = 197
CAP = 128
ROWS = 128
STREAMS = 2
EPS = 1e-06
BF = jnp.bfloat16
F32 = jnp.float32


def dot(spec, left, right):
    return jnp.einsum(spec, left, right, preferred_element_type=F32)


def swap(values):
    return lax.ppermute(values, "tensor", [(0, 1), (1, 0)])


def join_halves(own):
    return jnp.concatenate([own, swap(own)], axis=1)


def sum_halves(full, wire):
    rows = full.shape[1] // 2
    return full[:, :rows].astype(F32) + swap(full[:, rows:].astype(wire)).astype(F32)


def norm_stats(values):
    centre = values - jnp.mean(values, axis=-1, keepdims=True)
    inv = lax.rsqrt(jnp.mean(centre * centre, axis=-1, keepdims=True) + EPS)
    return centre * inv, inv


def norm_back(grad, unit, inv, gain):
    scaled = grad * gain
    return (
        scaled
        - jnp.mean(scaled, axis=-1, keepdims=True)
        - unit * jnp.mean(scaled * unit, axis=-1, keepdims=True)
    ) * inv


def gelu_parts(pre):
    inner = 0.7978845608028654 * (pre + 0.044715 * pre * pre * pre)
    return jnp.tanh(inner)


def forward(section_input, weights, tables):
    gain1, bias1, gain2, bias2, qkv, projt, router, inner, outert = weights
    onehot, kept, hot, key_live, = tables
    images, rows, features = section_input.shape
    length = 2 * rows
    experts = router.shape[1]
    heads = qkv.shape[2] // HEAD_DIM
    z = section_input.astype(F32)
    unit1, inv1 = norm_stats(z)
    a1 = join_halves((unit1 * gain1 + bias1).astype(BF))
    qkv_rows = dot("isd,jde->jise", a1, qkv).astype(BF)
    q, k, v = (qkv_rows[j].reshape(images, length, heads, HEAD_DIM) for j in range(3))
    scores = dot("iqhd,ikhd->ihqk", q, k) * HEAD_DIM**-0.5
    scores = jnp.where(key_live, scores, -1e30)
    top = jnp.max(scores, axis=-1, keepdims=True)
    weights_exp = jnp.exp(scores - top)
    probs = weights_exp / jnp.sum(weights_exp, axis=-1, keepdims=True)
    attended = dot("ihqk,ikhd->iqhd", probs.astype(BF), v).astype(BF)
    attended = attended.reshape(images, length, heads * HEAD_DIM)
    h1 = z + sum_halves(dot("ise,de->isd", attended, projt), F32)
    unit2, inv2 = norm_stats(h1)
    a2 = join_halves((unit2 * gain2 + bias2).astype(BF))
    router_probs = jax.nn.softmax(dot("isd,de->ise", a2, router), axis=-1)
    gate = jnp.sum(jnp.where(hot, router_probs[:, None], 0.0), axis=-1)
    dispatch = onehot[:, 0] + onehot[:, 1]
    rows_e = dot("isc,isd->icd", dispatch, a2).astype(BF)
    rows_e = rows_e.reshape(images, experts, CAP, features).transpose(1, 0, 2, 3)
    rows_e = rows_e.reshape(experts, images * CAP, features)
    pre = dot("ecd,edf->ecf", rows_e, inner)
    act = (0.5 * pre * (1.0 + gelu_parts(pre))).astype(BF)
    out = dot("ecf,edf->ecd", act, outert).astype(BF)
    out = out.reshape(experts, images, CAP, features).transpose(1, 0, 2, 3)
    out = out.reshape(images, experts * CAP, features)
    chosen = dot("iksc,icd->iksd", onehot, out)
    moe = jnp.sum(chosen * gate[..., None], axis=1)
    y = h1 + sum_halves(moe, F32)
    saved = (unit1, inv1, a1, q, k, v, probs, attended, unit2, inv2, a2, router_probs, gate,
             rows_e, pre, act, chosen.astype(BF))
    return y.astype(BF), saved


def backward(dy, saved, weights, tables, weight_grads):
    gain1, bias1, gain2, bias2, qkv, projt, router, inner, outert = weights
    onehot, kept, hot, key_live, = tables
    (unit1, inv1, a1, q, k, v, probs, attended, unit2, inv2, a2, router_probs, gate,
     rows_e, pre, act, chosen) = saved
    images, rows, features = dy.shape
    length = 2 * rows
    experts = router.shape[1]
    heads = qkv.shape[2] // HEAD_DIM
    scale = HEAD_DIM**-0.5
    grad_full = join_halves(dy).astype(F32)
    weighted = (gate[..., None] * grad_full[:, None]).astype(BF)
    dexp = dot("iksc,iksd->icd", onehot, weighted).astype(BF)
    dexp = dexp.reshape(images, experts, CAP, features).transpose(1, 0, 2, 3)
    dexp = dexp.reshape(experts, images * CAP, features)
    grad_outert = dot("ecd,ecf->edf", dexp, act).astype(BF)
    if weight_grads:
        grad_outert, dexp = lax.optimization_barrier((grad_outert, dexp))
    grad_act = dot("ecd,edf->ecf", dexp, outert)
    tanh = gelu_parts(pre)
    slope = 0.5 * (1.0 + tanh) + 0.5 * pre * (1.0 - tanh * tanh) * (
        0.7978845608028654 * (1.0 + 3 * 0.044715 * pre * pre)
    )
    dpre = (grad_act * slope).astype(BF)
    grad_inner = dot("ecd,ecf->edf", rows_e, dpre).astype(BF)
    if weight_grads:
        grad_inner, dpre = lax.optimization_barrier((grad_inner, dpre))
    drows = dot("ecf,edf->ecd", dpre, inner).astype(BF)
    drows = drows.reshape(experts, images, CAP, features).transpose(1, 0, 2, 3)
    drows = drows.reshape(images, experts * CAP, features)
    dgate = jnp.where(kept, jnp.sum(grad_full[:, None] * chosen.astype(F32), axis=-1), 0.0)
    drouter = jnp.sum(jnp.where(hot, dgate[..., None], 0.0), axis=1)
    dlogit = router_probs * (drouter - jnp.sum(router_probs * drouter, axis=-1, keepdims=True))
    grad_router = jnp.einsum(
        "isd,ise->de", a2.astype(F32), dlogit, precision=lax.Precision.HIGHEST
    )
    da2 = jnp.einsum("ise,de->isd", dlogit, router.astype(F32), precision=lax.Precision.HIGHEST)
    da2 = da2 + dot("isc,icd->isd", onehot[:, 0] + onehot[:, 1], drows)
    da2 = sum_halves(da2, BF)
    grad_gain2 = jnp.sum(da2 * unit2, axis=(0, 1))
    grad_bias2 = jnp.sum(da2, axis=(0, 1))
    dh1 = dy.astype(F32) + norm_back(da2, unit2, inv2, gain2)
    dbranch = join_halves(dh1.astype(BF))
    grad_projt = dot("isd,ise->de", dbranch, attended).astype(BF)
    datt = dot("isd,de->ise", dbranch, projt).astype(BF)
    datt = datt.reshape(images, length, heads, HEAD_DIM)
    dv = dot("ihqk,iqhd->ikhd", probs.astype(BF), datt).astype(BF)
    dprobs = dot("iqhd,ikhd->ihqk", datt, v)
    dscores = probs * (dprobs - jnp.sum(probs * dprobs, axis=-1, keepdims=True))
    dscores = dscores.astype(BF)
    dq = (dot("ihqk,ikhd->iqhd", dscores, k) * scale).astype(BF)
    dk = (dot("ihqk,iqhd->ikhd", dscores, q) * scale).astype(BF)
    flat = tuple(part.reshape(images, length, heads * HEAD_DIM) for part in (dq, dk, dv))
    rings = None
    if weight_grads:
        rings = (RingScatter(grad_outert, False, STREAMS), RingScatter(grad_inner, True, STREAMS))
        for ring in rings:
            ring.advance()
            ring.advance()
        flat, rings[0].moving, rings[1].moving = lax.optimization_barrier(
            (flat, rings[0].moving, rings[1].moving)
        )
    grad_qkv = dot("isd,ise->de", a1, jnp.concatenate(flat, axis=2)).astype(BF)
    da1 = sum(dot("ise,de->isd", part, qkv[j]) for j, part in enumerate(flat))
    da1 = sum_halves(da1, BF)
    grad_gain1 = jnp.sum(da1 * unit1, axis=(0, 1))
    grad_bias1 = jnp.sum(da1, axis=(0, 1))
    dz = dh1 + norm_back(da1, unit1, inv1, gain1)
    small = jnp.concatenate(
        [jnp.stack([grad_gain1, grad_bias1, grad_gain2, grad_bias2], axis=1), grad_router], axis=1
    )
    return dz, grad_qkv, grad_projt, small, rings


def gather_dp(shard):
    return lax.all_gather(shard, "dp", axis=shard.ndim - 2, tiled=True)


def scatter_dp(full):
    return lax.psum_scatter(full, "dp", scatter_dimension=full.ndim - 2, tiled=True)


def ring_plan(count, forward_way):
    order = list(range(0, count, 2)) + list(range(count - 1 - count % 2, 0, -2))
    if not forward_way:
        order = order[::-1]
    links = [(order[i], order[(i + 1) % count]) for i in range(count)]
    behind = np.zeros((count, count), np.int32)
    for place, device in enumerate(order):
        for steps in range(count):
            behind[device, steps] = order[(place - steps) % count]
    row = jnp.asarray(behind)[lax.axis_index("dp")]
    return links, [row[steps] for steps in range(count)]


def ring_gather(shard, forward_way):
    count = lax.axis_size("dp")
    links, behind = ring_plan(count, forward_way)
    experts, depth, wide = shard.shape
    moving = shard[:, None]
    whole = jnp.zeros((experts, count, depth, wide), shard.dtype)
    whole = lax.dynamic_update_slice_in_dim(whole, moving, behind[0], 1)
    for step in range(1, count):
        moving = lax.ppermute(moving, "dp", links)
        whole = lax.dynamic_update_slice_in_dim(whole, moving, behind[step], 1)
    return whole.reshape(experts, count * depth, wide)


class RingScatter:
    def __init__(self, full, forward_way, streams):
        self.count = lax.axis_size("dp")
        self.links, self.behind = ring_plan(self.count, forward_way)
        experts, depth, wide = full.shape
        blocks = full.reshape(experts, self.count, depth // self.count, wide)
        part = experts // streams
        self.mine = [blocks[i * part:(i + 1) * part] for i in range(streams)]
        self.moving = [self.block(mine, 1) for mine in self.mine]
        self.step = 2

    def block(self, mine, step):
        place = self.behind[step % self.count]
        return lax.dynamic_index_in_dim(mine, place, 1, keepdims=False)

    def advance(self):
        sums = []
        for mine, moving in zip(self.mine, self.moving):
            came = lax.ppermute(moving, "dp", self.links).astype(F32)
            total = came + self.block(mine, self.step).astype(F32)
            sums.append(total.astype(BF) if self.step < self.count else total)
        self.moving = sums
        self.step += 1

    def finish(self):
        while self.step <= self.count:
            self.advance()
        return jnp.concatenate(self.moving, axis=0)


def body(
    images_in,
    out_grad,
    attn_gain,
    attn_bias,
    qkv_weight,
    proj_weight,
    moe_gain,
    moe_bias,
    router_weight,
    inner_weight,
    outer_weight,
    expert_ids,
    slot_ids,
):
    is_first = lax.axis_index("pipe") == 0
    side = lax.axis_index("tensor")
    micro, local, piece, features = images_in.shape
    images = micro * local
    shard, wide = qkv_weight.shape[2], qkv_weight.shape[3]
    experts = router_weight.shape[2]
    packed = jnp.concatenate(
        [qkv_weight[0, 0], qkv_weight[0, 1], qkv_weight[0, 2], proj_weight[0].T,
         jnp.stack([attn_gain[0], attn_bias[0], moe_gain[0], moe_bias[0]], axis=1),
         router_weight[0], jnp.zeros((shard, 128 - 4 - experts), BF)],
        axis=1,
    )
    packed = gather_dp(packed)
    inner = ring_gather(inner_weight[0], True)
    outert = ring_gather(outer_weight[0].transpose(0, 2, 1), False)
    qkv = jnp.stack([packed[:, j * wide:(j + 1) * wide] for j in range(3)])
    projt = packed[:, 3 * wide:4 * wide]
    smalls = packed[:, 4 * wide:]
    gain1, bias1, gain2, bias2 = (smalls[:, j].astype(F32) for j in range(4))
    router = smalls[:, 4:4 + experts]
    weights = (gain1, bias1, gain2, bias2, qkv, projt, router, inner, outert)

    def pad_rows(values, fill=0):
        return jnp.pad(
            values, ((0, 0), (0, ROWS - piece), (0, 0)), constant_values=fill
        )

    def local_order(table, fill):
        halves = table[0].reshape(images, 2, piece, 2)
        halves = jnp.where(side == 0, halves, halves[:, ::-1])
        halves = jnp.pad(
            halves, ((0, 0), (0, 0), (0, ROWS - piece), (0, 0)), constant_values=fill
        )
        return halves.reshape(images, 2 * ROWS, 2).transpose(0, 2, 1)

    routes = local_order(expert_ids, 0)
    slots = local_order(slot_ids, CAP)
    kept = slots < CAP
    codes = jnp.where(kept, routes * CAP + slots, -1)
    onehot = (codes[..., None] == jnp.arange(experts * CAP, dtype=jnp.int32)).astype(BF)
    hot = routes[..., None] == jnp.arange(experts, dtype=jnp.int32)
    index = jnp.arange(2 * ROWS, dtype=jnp.int32)
    half = jnp.where(side == 0, index // ROWS, 1 - index // ROWS)
    row = index % ROWS
    key_live = (row < piece) & (half * piece + row < LIVE)
    tables = (onehot, kept, hot, key_live)

    start = pad_rows(images_in.reshape(images, piece, features))
    last = pad_rows(out_grad.reshape(images, piece, features))
    early, _ = forward(start, weights, tables)
    received = lax.ppermute(early, "pipe", [(0, 1)])
    y, saved = forward(jnp.where(is_first, start, received), weights, tables)
    late = backward(last, saved, weights, tables, False)[0]
    received = lax.ppermute(late.astype(BF), "pipe", [(1, 0)])
    dz, grad_qkv, grad_projt, small, rings = backward(
        jnp.where(is_first, received, last), saved, weights, tables, True
    )
    outer_out, inner_out = (ring.finish() for ring in rings)
    packed_grads = jnp.concatenate(
        [grad_qkv, grad_projt, small.astype(BF),
         jnp.zeros((features, 128 - small.shape[1]), BF)],
        axis=1,
    )
    packed_out = scatter_dp(packed_grads).astype(F32)
    own_small = packed_out[:, 4 * wide:4 * wide + small.shape[1]]
    own_small = own_small + swap(own_small)

    def shape_out(values):
        return values[:, :piece].reshape(1, micro, local, piece, features)

    return (
        shape_out(y),
        shape_out(dz),
        own_small[:, 0][None],
        own_small[:, 1][None],
        jnp.stack([packed_out[:, j * wide:(j + 1) * wide] for j in range(3)])[None],
        packed_out[:, 3 * wide:4 * wide].T[None],
        own_small[:, 2][None],
        own_small[:, 3][None],
        own_small[:, 4:][None],
        inner_out[None],
        outer_out.transpose(0, 2, 1)[None],
    )


def solution(mesh):
    in_specs = (
        P(None, "dp", "tensor", None),
        P(None, "dp", "tensor", None),
        P("pipe", "dp"),
        P("pipe", "dp"),
        P("pipe", None, "dp", "tensor"),
        P("pipe", "tensor", "dp"),
        P("pipe", "dp"),
        P("pipe", "dp"),
        P("pipe", "dp", None),
        P("pipe", None, "dp", "tensor"),
        P("pipe", None, "tensor", "dp"),
        P("pipe", None, "dp", None, None),
        P("pipe", None, "dp", None, None),
    )
    out_specs = (
        P("pipe", None, "dp", "tensor", None),
        P("pipe", None, "dp", "tensor", None),
        P("pipe", "dp"),
        P("pipe", "dp"),
        P("pipe", None, "dp", "tensor"),
        P("pipe", "tensor", "dp"),
        P("pipe", "dp"),
        P("pipe", "dp"),
        P("pipe", "dp", None),
        P("pipe", None, "dp", "tensor"),
        P("pipe", None, "tensor", "dp"),
    )
    return jax.shard_map(body, mesh=mesh, in_specs=in_specs, out_specs=out_specs, check_vma=False)
```
